32 devices in a mesh: aa: 8 (over y, x, core), ba: 4 (over z).
Axes of the slice: x: 2, y: 2, z: 4, core: 2. Of those that a mesh axis runs over, the one named last changes fastest.
Arguments:
- pair_amplitude: bfloat16 [1024, 1024, 5, 128], P('aa', 'ba'), may hold values from -0.5 to 0.5
- row_amplitude: bfloat16 [1024, 2, 5, 128], P(('aa', 'ba')), may hold values from -0.5 to 0.5
- column_amplitude: bfloat16 [1024, 2, 5, 128], P(('ba', 'aa')), may hold values from -0.5 to 0.5
- row_integral: bfloat16 [1024, 3200], P(('aa', 'ba')), may hold values from -6 to 6
- column_integral: bfloat16 [1024, 3200], P(('ba', 'aa')), may hold values from -6 to 6
- step_integral: bfloat16 [2, 3200], replicated, may hold values from -6 to 6
- virtual_energy: float32 [1024], replicated, may hold values from 0.3 to 2
- occupied_energy: float32 [5], replicated, may hold values from -1.5 to -0.2
- step_energy: float32 [2], replicated, may hold values from 0.3 to 2
Outputs:
- row_residual: float32 [1024, 2, 5, 128], P(('aa', 'ba'))
- column_residual: float32 [1024, 2, 5, 128], P(('ba', 'aa'))
The draws below stay inside these ranges and needn't reach their ends.
All inputs are finite; a program needn't handle non-finite values.
Results may differ from the reference program's by a relative error of at most 0.0005.
Values may be sent and summed in bfloat16 or wider, within the bound.
No kernel may reach another device: no remote copies, remote signals or barrier semaphores. Data moves between devices by JAX's collectives and lax.ppermute only.
A program may use at most 128 MiB of HBM per device.

```python
import math
import jax
import jax.numpy as jnp
from jax import lax

NV = 1024
NO = 128
OT = 5
NC = 2


def steps_of(key, dims, split, low, high):
    gain, own = 1.0, jax.random.fold_in(key, 6)
    for axis_at, shards_of in split:
        heights = jnp.exp(jax.random.uniform(jax.random.fold_in(own, axis_at), (shards_of,), jnp.float32, low / len(split), high / len(split)))
        gain = gain * jnp.repeat(heights, dims[axis_at] // shards_of).reshape([-1 if axis == axis_at else 1 for axis in range(len(dims))])
    return gain


def gaussian(key, shape, scale, limit, split=(), held_as=jnp.bfloat16):
    gain = steps_of(key, shape, split, -0.22, 0.18) if split else 1.0
    entries = jax.random.normal(key, shape, jnp.float32) * scale * gain
    return jnp.minimum(jnp.maximum(entries, -limit), limit).astype(held_as)


def setup_inputs(seed: int = 0) -> dict:
    splits = jax.random.split(jax.random.key(seed), 10)
    pair_amplitude = gaussian(splits[0], (NV, NV, OT, NO), NO ** -0.5, 0.5, ((0, 8), (1, 4)))
    row_amplitude = gaussian(splits[1], (NV, NC, OT, NO), NO ** -0.5, 0.5, ((0, 32),))
    column_amplitude = gaussian(splits[2], (NV, NC, OT, NO), NO ** -0.5, 0.5, ((0, 32),))
    row_integral = gaussian(splits[3], (NV, NO * OT * OT), 1.0, 6.0, ((0, 32),))
    column_integral = gaussian(splits[4], (NV, NO * OT * OT), 1.0, 6.0, ((0, 32),))
    step_integral = gaussian(splits[5], (NC, NO * OT * OT), 1.0, 6.0)
    virtual_energy = jnp.clip(jax.random.uniform(splits[6], (NV,), jnp.float32, 0.3, 2.0), 0.3, 2.0)
    occupied_energy = jnp.clip(jax.random.uniform(splits[7], (OT,), jnp.float32, -1.5, -0.2), -1.5, -0.2)
    step_energy = jnp.clip(jax.random.uniform(splits[8], (NC,), jnp.float32, 0.3, 2.0), 0.3, 2.0)
    return dict(pair_amplitude=pair_amplitude, row_amplitude=row_amplitude, column_amplitude=column_amplitude, row_integral=row_integral, column_integral=column_integral, step_integral=step_integral, virtual_energy=virtual_energy, occupied_energy=occupied_energy, step_energy=step_energy)


def block_terms(pair_block, lead_step, lead_table, tail_step, tail_table, table, lead_energy, tail_energy, energy_c, occupied_sum):
    triples = jnp.einsum('abil,ljk->abijk', pair_block, table)
    triples = triples + jnp.einsum('abjl,lki->abijk', pair_block, table)
    triples = triples + jnp.einsum('ail,bljk->abijk', lead_step, tail_table)
    triples = triples + jnp.einsum('akl,blij->abijk', lead_step, tail_table)
    triples = triples + jnp.einsum('bjl,alki->abijk', tail_step, lead_table)
    triples = triples + jnp.einsum('bkl,alij->abijk', tail_step, lead_table)
    denominator = lead_energy[:, None, None, None, None] + tail_energy[None, :, None, None, None] + energy_c - occupied_sum[None, None]
    weighted = lax.optimization_barrier((triples / denominator).astype(jnp.bfloat16)).astype(jnp.float32)
    row_part = jnp.einsum('abijk,bljk->ail', weighted, tail_table)
    column_part = jnp.einsum('abijk,alki->bjl', weighted, lead_table)
    return (row_part, column_part)

def reference(pair_amplitude, row_amplitude, column_amplitude, row_integral, column_integral, step_integral, virtual_energy, occupied_energy, step_energy):
    block = min(64, NV)
    factor = 1.0 / (math.sqrt(NV) * OT)
    occupied_sum = occupied_energy[:, None, None] + occupied_energy[None, :, None] + occupied_energy[None, None, :]
    step_table = step_integral.reshape(NC, NO, OT, OT).astype(jnp.float32)
    lead_all = row_integral.reshape(NV, NO, OT, OT)
    tail_table = column_integral.reshape(NV, NO, OT, OT).astype(jnp.float32)
    row_steps = []
    column_steps = []
    for which in range(NC):
        tail_step = column_amplitude[:, which].astype(jnp.float32)
        lead_source = row_amplitude[:, which]

        def one_block(column_total, index):
            start = (index * block).astype(jnp.int32)
            pair_block = lax.dynamic_slice_in_dim(pair_amplitude, start, block, 0).astype(jnp.float32)
            lead_step = lax.dynamic_slice_in_dim(lead_source, start, block, 0).astype(jnp.float32)
            lead_table = lax.dynamic_slice_in_dim(lead_all, start, block, 0).astype(jnp.float32)
            lead_energy = lax.dynamic_slice_in_dim(virtual_energy, start, block, 0)
            row_part, column_part = block_terms(pair_block, lead_step, lead_table, tail_step, tail_table, step_table[which], lead_energy, virtual_energy, step_energy[which], occupied_sum)
            return (column_total + column_part, row_part)
        column_total, row_parts = lax.scan(one_block, jnp.zeros((NV, OT, NO), jnp.float32), jnp.arange(NV // block, dtype=jnp.int32))
        row_steps.append(row_parts.reshape(NV, OT, NO))
        column_steps.append(column_total)
    row_residual = jnp.stack(row_steps, 1) * factor
    column_residual = jnp.stack(column_steps, 1) * factor
    return (row_residual, column_residual)
```

```python
import math

import jax
import jax.numpy as jnp
from jax import lax
from jax.experimental import pallas as pl
from jax.experimental.pallas import tpu as pltpu
from jax.sharding import PartitionSpec as P

VMEM = pl.BlockSpec(memory_space=pltpu.VMEM)
SMEM = pl.BlockSpec(memory_space=pltpu.SMEM)
TRANSPOSED = (((1,), (1,)), ((), ()))


def pack_kernel(amplitude, integral, packed, turned, *, lead, pairs, size):
    packed[0:lead] = amplitude[...]
    for part in range(pairs):
        piece = integral[:, part * size : (part + 1) * size].astype(jnp.float32)
        turned[part * size : (part + 1) * size, :] = piece.T
    for part in range(pairs):
        piece = turned[pl.ds(part, size, stride=pairs), :]
        packed[lead + part] = piece.T.astype(packed.dtype)


def pack(amplitude, integral):
    rows, steps, tile, size = amplitude.shape
    lead, pairs = steps * tile, tile * tile
    ordered = amplitude.transpose(1, 2, 0, 3).reshape(lead, rows, size)
    return pl.pallas_call(
        lambda *refs: pack_kernel(*refs, lead=lead, pairs=pairs, size=size),
        in_specs=[VMEM, VMEM],
        out_specs=VMEM,
        out_shape=jax.ShapeDtypeStruct((lead + pairs, rows, size), amplitude.dtype),
        scratch_shapes=[pltpu.VMEM((pairs * size, rows), jnp.float32)],
        compiler_params=pltpu.CompilerParams(vmem_limit_bytes=8 << 20),
        name="pack",
    )(ordered, integral)


def pair_kernel(table, pair, out, *, count, tile, block):
    first = pl.program_id(0) * block
    for i in range(tile):
        for at in range(block):
            product = lax.dot_general(
                table[...], pair[at, i], TRANSPOSED, preferred_element_type=jnp.float32
            )
            out[:, i, first + at, :] = product[:count]


def pair_product(table, pair):
    count, size = table.shape
    rows, tile, columns, _ = pair.shape
    block = math.gcd(rows, 8)
    padded = jnp.pad(table, ((0, -count % 8), (0, 0)))
    return pl.pallas_call(
        lambda *refs: pair_kernel(*refs, count=count, tile=tile, block=block),
        grid=(rows // block,),
        in_specs=[
            pl.BlockSpec(padded.shape, lambda g: (0, 0)),
            pl.BlockSpec((block, tile, columns, size), lambda g: (g, 0, 0, 0)),
        ],
        out_specs=VMEM,
        out_shape=pltpu.VMEM((count, tile, rows, columns), jnp.float32),
        compiler_params=pltpu.CompilerParams(vmem_limit_bytes=10 << 20),
        name="pair_product",
    )(padded, pair)


def place(parts, places, first, out):
    rows = parts[0].shape[1]
    for at, part in enumerate(parts):
        if len(parts) == 1:
            out[...] = part[...]
        else:
            start = pl.multiple_of(places[first + at] * rows, rows)
            out[:, pl.ds(start, rows), :] = part[...]


def triples_kernel(*refs, peers_a, peers_b, steps, tile, factor):
    lead_in, tail_in, refs = (
        refs[:peers_a], refs[peers_a : peers_a + peers_b], refs[peers_a + peers_b :]
    )
    (
        places, z, row_energy, column_energy, step_energy, occupied, row_out, column_out,
        lead, tail, lead_turned, tail_plain, inverse, column_total,
    ) = refs
    f32 = jnp.float32
    base = steps * tile
    pairs = tile * tile

    place(lead_in, places, 0, lead)
    place(tail_in, places, peers_a, tail_plain)

    @pl.loop(0, base + pairs)
    def _(e):
        tail[e] = tail_plain[e].T

    @pl.loop(0, pairs)
    def _(e):
        lead_turned[e] = lead[base + e].T

    row_out[...] = jnp.zeros_like(row_out)
    column_total[...] = jnp.zeros_like(column_total)

    def slot(i, j, k):
        low = jnp.minimum(jnp.minimum(i, j), k)
        high = jnp.maximum(jnp.maximum(i, j), k)
        middle = i + j + k - low - high
        return high * (high + 1) * (high + 2) // 6 + middle * (middle + 1) // 2 + low

    @pl.loop(0, steps)
    def _(s):
        virtual = row_energy[...] + column_energy[...] + step_energy[s]
        at = 0
        for high in range(tile):
            for middle in range(high + 1):
                for low in range(middle + 1):
                    inverse[at] = 1.0 / (
                        virtual - (occupied[low] + occupied[middle] + occupied[high])
                    )
                    at += 1

        @pl.loop(0, pairs)
        def _(ij):
            i = ij // tile
            j = ij % tile
            lead_i = lead[s * tile + i]
            lead_ij = lead[base + ij]
            tail_j = tail[s * tile + j]
            tail_ij = tail[base + ij]
            parts = []
            for k in range(tile):
                left = jnp.concatenate(
                    [lead_i, lead[s * tile + k], lead[base + k * tile + i], lead_ij], axis=1
                )
                right = jnp.concatenate(
                    [tail[base + j * tile + k], tail_ij, tail_j, tail[s * tile + k]], axis=0
                )
                w = jnp.dot(left, right, preferred_element_type=f32)
                w = w + z[s * pairs + j * tile + k, i] + z[s * pairs + k * tile + i, j]
                parts.append((w * inverse[slot(i, j, k)]).astype(left.dtype))
            table = tail_plain[pl.ds(base + j * tile, tile)]
            row_out[s * tile + i] += jnp.dot(
                jnp.concatenate(parts, axis=1),
                table.reshape(tile * table.shape[1], table.shape[2]),
                preferred_element_type=f32,
            )
            column_total[s * tile + j] += jnp.dot(
                jnp.concatenate([lead_turned[k * tile + i] for k in range(tile)], axis=1),
                jnp.concatenate(parts, axis=0),
                preferred_element_type=f32,
            )

    row_out[...] = row_out[...] * factor

    @pl.loop(0, base)
    def _(e):
        column_out[e] = column_total[e].T * factor


def triples(z, lead_in, tail_in, places, row_energy, column_energy, step_energy, occupied, factor):
    _, tile, rows, columns = z.shape
    steps = step_energy.shape[0]
    kinds, _, size = lead_in[0].shape
    base, pairs = steps * tile, tile * tile
    f32, kept = jnp.float32, lead_in[0].dtype
    peers_a, peers_b = len(lead_in), len(tail_in)
    distinct = tile * (tile + 1) * (tile + 2) // 6
    return pl.pallas_call(
        lambda *refs: triples_kernel(
            *refs, peers_a=peers_a, peers_b=peers_b, steps=steps, tile=tile, factor=factor
        ),
        in_specs=[VMEM] * (peers_a + peers_b) + [SMEM] + [VMEM] * 3 + [SMEM] * 2,
        out_specs=[VMEM] * 2,
        out_shape=[
            jax.ShapeDtypeStruct((base, rows, size), f32),
            jax.ShapeDtypeStruct((base, columns, size), f32),
        ],
        scratch_shapes=[
            pltpu.VMEM((kinds, rows, size), kept),
            pltpu.VMEM((kinds, size, columns), kept),
            pltpu.VMEM((pairs, size, rows), kept),
            pltpu.VMEM((kinds, columns, size), kept),
            pltpu.VMEM((distinct, rows, columns), f32),
            pltpu.VMEM((base, size, columns), f32),
        ],
        compiler_params=pltpu.CompilerParams(vmem_limit_bytes=15 << 20),
        name="triples",
    )(*lead_in, *tail_in, places, z, row_energy, column_energy, step_energy, occupied)


def gather(packed, axis):
    count = lax.axis_size(axis)
    if packed.shape[1] % 16 or count & (count - 1):
        return [lax.all_gather(packed, axis, axis=1, tiled=True)], [jnp.int32(0)]
    here = lax.axis_index(axis)
    parts, places = [packed], [here]
    for flip in range(1, count):
        parts.append(lax.ppermute(packed, axis, [(at, at ^ flip) for at in range(count)]))
        places.append(here ^ flip)
    return parts, places


def on_device(
    pair_amplitude,
    row_amplitude,
    column_amplitude,
    row_integral,
    column_integral,
    step_integral,
    virtual_energy,
    occupied_energy,
    step_energy,
):
    tile_rows, tile_columns, tile, size = pair_amplitude.shape
    steps = row_amplitude.shape[1]
    virtual_count = tile_rows * lax.axis_size("aa")
    factor = 1.0 / (math.sqrt(virtual_count) * tile)
    row_energy = lax.dynamic_slice_in_dim(
        virtual_energy, lax.axis_index("aa") * tile_rows, tile_rows
    )
    column_energy = lax.dynamic_slice_in_dim(
        virtual_energy, lax.axis_index("ba") * tile_columns, tile_columns
    )
    tail_in, tail_places = gather(pack(column_amplitude, column_integral), "aa")
    lead_in, lead_places = gather(pack(row_amplitude, row_integral), "ba")
    table = step_integral.reshape(steps, size, tile * tile).transpose(0, 2, 1)
    table = table.reshape(steps * tile * tile, size)
    places = jnp.stack(lead_places + tail_places)
    row_energy, column_energy = row_energy[:, None], column_energy[None, :]
    table, places, row_energy, column_energy = lax.optimization_barrier(
        (table, places, row_energy, column_energy)
    )
    z = pair_product(table, pair_amplitude.transpose(0, 2, 1, 3))
    row, column = triples(
        z, lead_in, tail_in, places, row_energy, column_energy, step_energy, occupied_energy,
        factor,
    )
    row = lax.psum_scatter(row, "ba", scatter_dimension=1, tiled=True)
    column = lax.psum_scatter(column, "aa", scatter_dimension=1, tiled=True)

    def ordered(part):
        return part.reshape(steps, tile, part.shape[1], size).transpose(2, 0, 1, 3)

    return ordered(row), ordered(column)


def solution(mesh):
    placed = (
        P("aa", "ba", None, None),
        P(("aa", "ba"), None, None, None),
        P(("ba", "aa"), None, None, None),
        P(("aa", "ba"), None),
        P(("ba", "aa"), None),
        P(),
        P(),
        P(),
        P(),
    )
    return jax.shard_map(
        on_device,
        mesh=mesh,
        in_specs=placed,
        out_specs=(P(("aa", "ba"), None, None, None), P(("ba", "aa"), None, None, None)),
        check_vma=False,
    )
```

```python
import math

import jax
import jax.numpy as jnp
from jax import lax
from jax.experimental import pallas as pl
from jax.experimental.pallas import tpu as pltpu
from jax.sharding import PartitionSpec as P

VMEM = pl.BlockSpec(memory_space=pltpu.VMEM)
SMEM = pl.BlockSpec(memory_space=pltpu.SMEM)
TRANSPOSED = (((1,), (1,)), ((), ()))


def pack_kernel(amplitude, integral, packed, turned, *, lead, pairs, size):
    packed[0:lead] = amplitude[...]
    for part in range(pairs):
        piece = integral[:, part * size : (part + 1) * size].astype(jnp.float32)
        turned[part * size : (part + 1) * size, :] = piece.T
    for part in range(pairs):
        piece = turned[pl.ds(part, size, stride=pairs), :]
        packed[lead + part] = piece.T.astype(packed.dtype)


def pack(amplitude, integral):
    rows, steps, tile, size = amplitude.shape
    lead, pairs = steps * tile, tile * tile
    ordered = amplitude.transpose(1, 2, 0, 3).reshape(lead, rows, size)
    return pl.pallas_call(
        lambda *refs: pack_kernel(*refs, lead=lead, pairs=pairs, size=size),
        in_specs=[VMEM, VMEM],
        out_specs=VMEM,
        out_shape=jax.ShapeDtypeStruct((lead + pairs, rows, size), amplitude.dtype),
        scratch_shapes=[pltpu.VMEM((pairs * size, rows), jnp.float32)],
        compiler_params=pltpu.CompilerParams(vmem_limit_bytes=8 << 20),
        name="pack",
    )(ordered, integral)


def pair_kernel(table, pair, out, *, count, tile, block, group):
    first = pl.program_id(0) * block
    for at in range(0, block, group):
        rows = pl.ds(pl.multiple_of(first + at, group), group)
        for i in range(tile):
            products = [
                lax.dot_general(
                    table[...], pair[at + row, i], TRANSPOSED, preferred_element_type=jnp.float32
                )
                for row in range(group)
            ]
            turned = jnp.swapaxes(jnp.stack(products, axis=0), 0, 1)
            out[:, i, rows, :] = turned[:count]


def pair_product(table, pair):
    count, size = table.shape
    rows, tile, columns, _ = pair.shape
    block, group = math.gcd(rows, 16), math.gcd(rows, 8)
    padded = jnp.pad(table, ((0, -count % 8), (0, 0)))
    return pl.pallas_call(
        lambda *refs: pair_kernel(*refs, count=count, tile=tile, block=block, group=group),
        grid=(rows // block,),
        in_specs=[
            pl.BlockSpec(padded.shape, lambda g: (0, 0)),
            pl.BlockSpec((block, tile, columns, size), lambda g: (g, 0, 0, 0)),
        ],
        out_specs=VMEM,
        out_shape=pltpu.VMEM((count, tile, rows, columns), jnp.float32),
        compiler_params=pltpu.CompilerParams(vmem_limit_bytes=14 << 20),
        name="pair_product",
    )(padded, pair)


def place(parts, places, first, out):
    rows = parts[0].shape[1]
    for at, part in enumerate(parts):
        if len(parts) == 1:
            out[...] = part[...]
        else:
            start = pl.multiple_of(places[first + at] * rows, rows)
            out[:, pl.ds(start, rows), :] = part[...]


def triples_kernel(*refs, peers_a, peers_b, steps, tile, factor):
    lead_in, tail_in, refs = (
        refs[:peers_a], refs[peers_a : peers_a + peers_b], refs[peers_a + peers_b :]
    )
    places, z, row_energy, column_energy, step_energy, occupied = refs[:6]
    row_out, column_out = refs[6 : 6 + peers_a], refs[6 + peers_a : -8]
    (
        lead, tail, lead_turned, tail_plain, inverse, row_total, column_total, column_turned,
    ) = refs[-8:]
    f32 = jnp.float32
    base = steps * tile
    pairs = tile * tile

    place(lead_in, places, 0, lead)
    place(tail_in, places, peers_a, tail_plain)

    @pl.loop(0, base + pairs)
    def _(e):
        tail[e] = tail_plain[e].T

    @pl.loop(0, pairs)
    def _(e):
        lead_turned[e] = lead[base + e].T

    row_total[...] = jnp.zeros_like(row_total)
    column_total[...] = jnp.zeros_like(column_total)

    def slot(i, j, k):
        low = jnp.minimum(jnp.minimum(i, j), k)
        high = jnp.maximum(jnp.maximum(i, j), k)
        middle = i + j + k - low - high
        return high * (high + 1) * (high + 2) // 6 + middle * (middle + 1) // 2 + low

    @pl.loop(0, steps)
    def _(s):
        virtual = row_energy[...] + column_energy[...] + step_energy[s]
        at = 0
        for high in range(tile):
            for middle in range(high + 1):
                for low in range(middle + 1):
                    inverse[at] = 1.0 / (
                        virtual - (occupied[low] + occupied[middle] + occupied[high])
                    )
                    at += 1

        def forward(i, j):
            lead_i = lead[s * tile + i]
            lead_ij = lead[base + i * tile + j]
            tail_j = tail[s * tile + j]
            tail_ij = tail[base + i * tile + j]
            parts = []
            for k in range(tile):
                left = jnp.concatenate(
                    [lead_i, lead[s * tile + k], lead[base + k * tile + i], lead_ij], axis=1
                )
                right = jnp.concatenate(
                    [tail[base + j * tile + k], tail_ij, tail_j, tail[s * tile + k]], axis=0
                )
                w = jnp.dot(left, right, preferred_element_type=f32)
                w = w + z[s * pairs + j * tile + k, i] + z[s * pairs + k * tile + i, j]
                parts.append((w * inverse[slot(i, j, k)]).astype(left.dtype))
            return parts

        def back(parts, i, j):
            table = tail_plain[pl.ds(base + j * tile, tile)]
            row_total[s * tile + i] += jnp.dot(
                jnp.concatenate(parts, axis=1),
                table.reshape(tile * table.shape[1], table.shape[2]),
                preferred_element_type=f32,
            )
            column_total[s * tile + j] += jnp.dot(
                jnp.concatenate([lead_turned[k * tile + i] for k in range(tile)], axis=1),
                jnp.concatenate(parts, axis=0),
                preferred_element_type=f32,
            )

        @pl.loop(0, tile)
        def _(i):
            waiting = None
            for j in range(tile):
                parts = forward(i, j)
                if j:
                    back(waiting, i, j - 1)
                waiting = parts
            back(waiting, i, tile - 1)

    @pl.loop(0, base)
    def _(e):
        column_turned[e] = column_total[e].T

    hand_out(row_total, row_out, places, 0, factor)
    if peers_b == 1:
        column_out[0][...] = column_turned[...] * factor
    else:
        for at in range(peers_b // 2):
            for side, out in enumerate(column_out):
                rows = out.shape[2]
                start = pl.multiple_of(places[peers_a + 2 * at + side] * rows, rows)
                out[at] = column_turned[:, pl.ds(start, rows), :] * factor


def hand_out(total, outs, places, first, factor):
    for at, out in enumerate(outs):
        if len(outs) == 1:
            out[...] = total[...] * factor
        else:
            rows = out.shape[1]
            start = pl.multiple_of(places[first + at] * rows, rows)
            out[...] = total[:, pl.ds(start, rows), :] * factor


def triples(z, lead_in, tail_in, places, row_energy, column_energy, step_energy, occupied, factor):
    _, tile, rows, columns = z.shape
    steps = step_energy.shape[0]
    kinds, _, size = lead_in[0].shape
    base, pairs = steps * tile, tile * tile
    f32, kept = jnp.float32, lead_in[0].dtype
    peers_a, peers_b = len(lead_in), len(tail_in)
    distinct = tile * (tile + 1) * (tile + 2) // 6
    column_shapes = [(base, columns, size)]
    if peers_b > 1:
        column_shapes = [(peers_b // 2, base, columns // peers_b, size)] * 2
    outs = pl.pallas_call(
        lambda *refs: triples_kernel(
            *refs, peers_a=peers_a, peers_b=peers_b, steps=steps, tile=tile, factor=factor
        ),
        in_specs=[VMEM] * (peers_a + peers_b) + [SMEM] + [VMEM] * 3 + [SMEM] * 2,
        out_specs=[VMEM] * (peers_a + len(column_shapes)),
        out_shape=[jax.ShapeDtypeStruct((base, rows // peers_a, size), f32)] * peers_a
        + [jax.ShapeDtypeStruct(shape, f32) for shape in column_shapes],
        scratch_shapes=[
            pltpu.VMEM((kinds, rows, size), kept),
            pltpu.VMEM((kinds, size, columns), kept),
            pltpu.VMEM((pairs, size, rows), kept),
            pltpu.VMEM((kinds, columns, size), kept),
            pltpu.VMEM((distinct, rows, columns), f32),
            pltpu.VMEM((base, rows, size), f32),
            pltpu.VMEM((base, size, columns), f32),
            pltpu.VMEM((base, columns, size), f32),
        ],
        compiler_params=pltpu.CompilerParams(vmem_limit_bytes=15 << 20),
        name="triples",
    )(*lead_in, *tail_in, places, z, row_energy, column_energy, step_energy, occupied)
    return list(outs[:peers_a]), list(outs[peers_a:])


def halve(kept, came):
    count = kept.shape[0]

    def kernel(kept, came, *outs):
        for at, out in enumerate(outs):
            out[...] = kept[at] + came[at]

    return pl.pallas_call(
        kernel,
        in_specs=[VMEM] * 2,
        out_specs=[VMEM] * count,
        out_shape=[jax.ShapeDtypeStruct(kept.shape[1:], kept.dtype)] * count,
        compiler_params=pltpu.CompilerParams(vmem_limit_bytes=8 << 20),
        name="halve",
    )(kept, came)


def finish(row_parts, column_parts, steps, tile):
    _, rows_a, size = row_parts[0].shape
    rows_b = column_parts[0].shape[1]
    count = len(row_parts)

    def kernel(*refs):
        ins, outs = refs[:-2], refs[-2:]
        for parts, out in zip((ins[:count], ins[count:]), outs):
            for s in range(steps):
                for i in range(tile):
                    total = parts[0][s * tile + i]
                    for part in parts[1:]:
                        total = total + part[s * tile + i]
                    out[:, i, s, :] = total

    outs = pl.pallas_call(
        kernel,
        in_specs=[VMEM] * (count + len(column_parts)),
        out_specs=[VMEM] * 2,
        out_shape=[
            jax.ShapeDtypeStruct((rows, tile, steps, size), jnp.float32)
            for rows in (rows_a, rows_b)
        ],
        compiler_params=pltpu.CompilerParams(vmem_limit_bytes=8 << 20),
        name="finish",
    )(*row_parts, *column_parts)
    return [out.transpose(0, 2, 1, 3) for out in outs]


def send(part, axis, flip):
    count = lax.axis_size(axis)
    return lax.ppermute(part, axis, [(at, at ^ flip) for at in range(count)])


def scatter_row(parts):
    if len(parts) == 1:
        return [lax.psum_scatter(parts[0], "ba", scatter_dimension=1, tiled=True)]
    return parts[:1] + [send(part, "ba", flip) for flip, part in enumerate(parts) if flip]


def scatter_column(parts):
    if len(parts) == 1:
        return [lax.psum_scatter(parts[0], "aa", scatter_dimension=1, tiled=True)]
    parts = list(halve(parts[0], send(parts[1], "aa", 1)))
    return parts[:1] + [send(part, "aa", 2 * at) for at, part in enumerate(parts) if at]


def gather(packed, axis):
    count = lax.axis_size(axis)
    if packed.shape[1] % 16 or count & (count - 1):
        return [lax.all_gather(packed, axis, axis=1, tiled=True)], [jnp.int32(0)]
    here = lax.axis_index(axis)
    parts, places = [packed], [here]
    for flip in range(1, count):
        parts.append(send(packed, axis, flip))
        places.append(here ^ flip)
    return parts, places


def on_device(
    pair_amplitude,
    row_amplitude,
    column_amplitude,
    row_integral,
    column_integral,
    step_integral,
    virtual_energy,
    occupied_energy,
    step_energy,
):
    tile_rows, tile_columns, tile, size = pair_amplitude.shape
    steps = row_amplitude.shape[1]
    virtual_count = tile_rows * lax.axis_size("aa")
    factor = 1.0 / (math.sqrt(virtual_count) * tile)
    row_energy = lax.dynamic_slice_in_dim(
        virtual_energy, lax.axis_index("aa") * tile_rows, tile_rows
    )
    column_energy = lax.dynamic_slice_in_dim(
        virtual_energy, lax.axis_index("ba") * tile_columns, tile_columns
    )
    tail_in, tail_places = gather(pack(column_amplitude, column_integral), "aa")
    lead_in, lead_places = gather(pack(row_amplitude, row_integral), "ba")
    table = step_integral.reshape(steps, size, tile * tile).transpose(0, 2, 1)
    table = table.reshape(steps * tile * tile, size)
    places = jnp.stack(lead_places + tail_places)
    row_energy, column_energy = row_energy[:, None], column_energy[None, :]
    table, places, row_energy, column_energy = lax.optimization_barrier(
        (table, places, row_energy, column_energy)
    )
    z = pair_product(table, pair_amplitude.transpose(0, 2, 1, 3))
    row, column = triples(
        z, lead_in, tail_in, places, row_energy, column_energy, step_energy, occupied_energy,
        factor,
    )
    return tuple(finish(scatter_row(row), scatter_column(column), steps, tile))


def solution(mesh):
    placed = (
        P("aa", "ba", None, None),
        P(("aa", "ba"), None, None, None),
        P(("ba", "aa"), None, None, None),
        P(("aa", "ba"), None),
        P(("ba", "aa"), None),
        P(),
        P(),
        P(),
        P(),
    )
    return jax.shard_map(
        on_device,
        mesh=mesh,
        in_specs=placed,
        out_specs=(P(("aa", "ba"), None, None, None), P(("ba", "aa"), None, None, None)),
        check_vma=False,
    )
```

```python
import math

import jax
import jax.numpy as jnp
from jax import lax
from jax.experimental import pallas as pl
from jax.experimental.pallas import tpu as pltpu
from jax.sharding import PartitionSpec as P

VMEM = pl.BlockSpec(memory_space=pltpu.VMEM)
SMEM = pl.BlockSpec(memory_space=pltpu.SMEM)
TRANSPOSED = (((1,), (1,)), ((), ()))


def part_by_pair(integral, turned, store, pairs, size):
    rows = integral.shape[0]
    for part in range(pairs):
        piece = integral[:, part * size : (part + 1) * size].astype(jnp.float32)
        turned[part * size : (part + 1) * size, :rows] = piece.T
    for part in range(pairs):
        store(part, turned[pl.ds(part, size, stride=pairs), :rows].T)


def pack_kernel(*refs, steps, tile, size):
    pairs = tile * tile
    given, packs, table, turned, copied, arrived = (
        refs[0:5], refs[5:7], refs[7], refs[8:11], refs[11:16], refs[16]
    )
    copies = [
        pltpu.make_async_copy(source, target, arrived.at[at])
        for at, (source, target) in enumerate(zip(given, copied))
    ]
    for copy in copies:
        copy.start()
    amplitudes, integrals, step_integral = copied[0:2], copied[2:4], copied[4]
    for side, (amplitude, integral, packed, scratch) in enumerate(
        zip(amplitudes, integrals, packs, turned)
    ):
        copies[side].wait()
        copies[2 + side].wait()
        for s in range(steps):
            for i in range(tile):
                packed[s * tile + i] = amplitude[:, i, s, :]

        def store(part, piece, packed=packed):
            packed[steps * tile + part] = piece.astype(packed.dtype)

        part_by_pair(integral, scratch, store, pairs, size)

    def store_table(part, piece):
        for s in range(steps):
            table[s * pairs + part] = piece[s].astype(table.dtype)

    copies[4].wait()
    part_by_pair(step_integral, turned[2], store_table, pairs, size)


def pack(row_amplitude, column_amplitude, row_integral, column_integral, step_integral):
    rows, steps, tile, size = row_amplitude.shape
    kinds, pairs = steps * tile + tile * tile, tile * tile
    kept = row_amplitude.dtype
    scratch = pltpu.VMEM((pairs * size, rows), jnp.float32)
    count = steps * pairs
    given = (
        row_amplitude.transpose(0, 2, 1, 3), column_amplitude.transpose(0, 2, 1, 3),
        row_integral, column_integral, step_integral,
    )
    return pl.pallas_call(
        lambda *refs: pack_kernel(*refs, steps=steps, tile=tile, size=size),
        in_specs=[pl.BlockSpec(memory_space=pltpu.HBM)] * 5,
        out_specs=[VMEM] * 3,
        out_shape=[jax.ShapeDtypeStruct((kinds, rows, size), kept)] * 2
        + [jax.ShapeDtypeStruct((count + -count % 8, size), kept)],
        scratch_shapes=[scratch, scratch, pltpu.VMEM((pairs * size, steps), jnp.float32)]
        + [pltpu.VMEM(each.shape, kept) for each in given]
        + [pltpu.SemaphoreType.DMA((5,))],
        compiler_params=pltpu.CompilerParams(vmem_limit_bytes=14 << 20),
        name="pack",
    )(*[pltpu.with_memory_space_constraint(each, pltpu.HBM) for each in given])


def pair_kernel(table, pair, out, *, count, tile, block, group):
    first = pl.program_id(0) * block
    for at in range(0, block, group):
        rows_here = pl.ds(pl.multiple_of(first + at, group), group)
        for i in range(tile):
            products = [
                lax.dot_general(
                    table[...], pair[at + row, i], TRANSPOSED, preferred_element_type=jnp.float32
                )
                for row in range(group)
            ]
            turned = jnp.swapaxes(jnp.stack(products, axis=0), 0, 1)
            out[:, i, rows_here, :] = turned[:count]


def pair_product(table, pair, steps):
    rows, tile, columns, size = pair.shape
    count = steps * tile * tile
    block, group = math.gcd(rows, 16), math.gcd(rows, 8)
    return pl.pallas_call(
        lambda *refs: pair_kernel(*refs, count=count, tile=tile, block=block, group=group),
        grid=(rows // block,),
        in_specs=[
            pl.BlockSpec(table.shape, lambda g: (0, 0)),
            pl.BlockSpec((block, tile, columns, size), lambda g: (g, 0, 0, 0)),
        ],
        out_specs=VMEM,
        out_shape=pltpu.VMEM((count, tile, rows, columns), jnp.float32),
        compiler_params=pltpu.CompilerParams(vmem_limit_bytes=14 << 20),
        name="pair_product",
    )(table, pair)


def place(parts, places, first, out):
    rows = parts[0].shape[1]
    for at, part in enumerate(parts):
        if len(parts) == 1:
            out[...] = part[...]
        else:
            start = pl.multiple_of(places[first + at] * rows, rows)
            out[:, pl.ds(start, rows), :] = part[...]


def triples_kernel(*refs, peers_a, peers_b, steps, tile, factor):
    lead_in, tail_in, refs = (
        refs[:peers_a], refs[peers_a : peers_a + peers_b], refs[peers_a + peers_b :]
    )
    places, step_energy, occupied, energies, z = refs[:5]
    row_out, column_out = refs[5 : 5 + peers_a], refs[5 + peers_a : -8]
    (
        lead, tail, lead_turned, tail_plain, inverse, row_total, column_total, carried,
    ) = refs[-8:]
    f32 = jnp.float32
    base = steps * tile
    pairs = tile * tile

    place(lead_in, places, 2, lead)
    place(tail_in, places, 2 + peers_a, tail_plain)

    @pl.loop(0, base + pairs, unroll=tile)
    def _(e):
        tail[e] = tail_plain[e].T

    @pl.loop(0, pairs, unroll=tile)
    def _(e):
        lead_turned[e] = lead[base + e].T

    row_total[...] = jnp.zeros_like(row_total)
    column_total[...] = jnp.zeros_like(column_total)

    def slot(i, j, k):
        low = jnp.minimum(jnp.minimum(i, j), k)
        high = jnp.maximum(jnp.maximum(i, j), k)
        middle = i + j + k - low - high
        return high * (high + 1) * (high + 2) // 6 + middle * (middle + 1) // 2 + low

    def forward(s, i, j):
        lead_i = lead[s * tile + i]
        lead_ij = lead[base + i * tile + j]
        tail_j = tail[s * tile + j]
        tail_ij = tail[base + i * tile + j]
        parts = []
        for k in range(tile):
            left = jnp.concatenate(
                [lead_i, lead[s * tile + k], lead[base + k * tile + i], lead_ij], axis=1
            )
            right = jnp.concatenate(
                [tail[base + j * tile + k], tail_ij, tail_j, tail[s * tile + k]], axis=0
            )
            w = jnp.dot(left, right, preferred_element_type=f32)
            w = w + z[s * pairs + j * tile + k, i] + z[s * pairs + k * tile + i, j]
            parts.append((w * inverse[slot(i, j, k)]).astype(left.dtype))
        return parts

    def back(parts, s, i, j):
        table = tail_plain[pl.ds(base + j * tile, tile)]
        row_total[s * tile + i] += jnp.dot(
            jnp.concatenate(parts, axis=1),
            table.reshape(tile * table.shape[1], table.shape[2]),
            preferred_element_type=f32,
        )
        column_total[s * tile + j] += jnp.dot(
            jnp.concatenate([lead_turned[k * tile + i] for k in range(tile)], axis=1),
            jnp.concatenate(parts, axis=0),
            preferred_element_type=f32,
        )

    carried[...] = jnp.zeros_like(carried)

    rows, columns = z.shape[2:]
    unit = energies.shape[1]

    def energy(first, count):
        return [energies[pl.ds(first + piece, 1), :] for piece in range(count)]

    diagonal = lax.broadcasted_iota(jnp.int32, (unit, unit), 0) == lax.broadcasted_iota(
        jnp.int32, (unit, unit), 1
    )
    upright = [
        jnp.sum(jnp.where(diagonal, piece, 0.0), axis=1, keepdims=True)
        for piece in energy(places[0] * (rows // unit), rows // unit)
    ]
    across = energy(places[1] * (columns // unit), columns // unit)
    virtual = jnp.concatenate(upright, axis=0) + jnp.concatenate(across, axis=1)

    @pl.loop(0, steps)
    def _(s):
        at = 0
        for high in range(tile):
            for middle in range(high + 1):
                for low in range(middle + 1):
                    hole = occupied[low] + occupied[middle] + occupied[high]
                    inverse[at] = 1.0 / (virtual + step_energy[s] - hole)
                    at += 1

        @pl.loop(0, tile)
        def _(i):
            before = jnp.maximum(s * tile + i - 1, 0)
            waiting = [carried[k] for k in range(tile)]
            for j in range(tile):
                parts = forward(s, i, j)
                if j:
                    back(waiting, s, i, j - 1)
                else:
                    back(waiting, before // tile, before % tile, tile - 1)
                waiting = parts
            for k in range(tile):
                carried[k] = waiting[k]

    back([carried[k] for k in range(tile)], steps - 1, tile - 1, tile - 1)

    hand_out(row_total, row_out, places, 2, factor)
    if peers_b == 1:
        for e in range(base):
            column_out[0][e] = column_total[e].T * factor
        return
    rows = column_out[0].shape[2]
    here = places[2 + peers_a]

    def hand_out_columns(parity):
        @pl.loop(0, base, unroll=tile)
        def _(e):
            turned = column_total[e].T * factor
            for peer in range(peers_b):
                out = column_out[(peer + parity) % 2]
                out[(here ^ peer) // 2, e] = turned[peer * rows : (peer + 1) * rows]

    for parity in range(2):
        pl.when(here % 2 == parity)(lambda parity=parity: hand_out_columns(parity))


def hand_out(total, outs, places, first, factor):
    for at, out in enumerate(outs):
        if len(outs) == 1:
            out[...] = total[...] * factor
        else:
            rows = out.shape[1]
            start = pl.multiple_of(places[first + at] * rows, rows)
            out[...] = total[:, pl.ds(start, rows), :] * factor


def triples(places, step_energy, occupied, energies, z, lead_in, tail_in, factor):
    _, tile, rows, columns = z.shape
    steps = step_energy.shape[0]
    distinct = tile * (tile + 1) * (tile + 2) // 6
    kinds, _, size = lead_in[0].shape
    base, pairs = steps * tile, tile * tile
    f32, kept = jnp.float32, lead_in[0].dtype
    peers_a, peers_b = len(lead_in), len(tail_in)
    column_shapes = [(base, columns, size)]
    if peers_b > 1:
        column_shapes = [(peers_b // 2, base, columns // peers_b, size)] * 2
    outs = pl.pallas_call(
        lambda *refs: triples_kernel(
            *refs, peers_a=peers_a, peers_b=peers_b, steps=steps, tile=tile, factor=factor
        ),
        in_specs=[VMEM] * (peers_a + peers_b) + [SMEM] * 3 + [VMEM] * 2,
        out_specs=[VMEM] * (peers_a + len(column_shapes)),
        out_shape=[jax.ShapeDtypeStruct((base, rows // peers_a, size), f32)] * peers_a
        + [jax.ShapeDtypeStruct(shape, f32) for shape in column_shapes],
        scratch_shapes=[
            pltpu.VMEM((kinds, rows, size), kept),
            pltpu.VMEM((kinds, size, columns), kept),
            pltpu.VMEM((pairs, size, rows), kept),
            pltpu.VMEM((kinds, columns, size), kept),
            pltpu.VMEM((distinct, rows, columns), f32),
            pltpu.VMEM((base, rows, size), f32),
            pltpu.VMEM((base, size, columns), f32),
            pltpu.VMEM((tile, rows, columns), kept),
        ],
        compiler_params=pltpu.CompilerParams(vmem_limit_bytes=15 << 20),
        name="triples",
    )(*lead_in, *tail_in, places, step_energy, occupied, energies, z)
    return list(outs[:peers_a]), list(outs[peers_a:])


def halve(kept, came):
    count = kept.shape[0]

    def kernel(kept, came, *outs):
        for at, out in enumerate(outs):
            out[...] = kept[at] + came[at]

    return pl.pallas_call(
        kernel,
        in_specs=[VMEM] * 2,
        out_specs=[VMEM] * count,
        out_shape=[jax.ShapeDtypeStruct(kept.shape[1:], kept.dtype)] * count,
        compiler_params=pltpu.CompilerParams(vmem_limit_bytes=8 << 20),
        name="halve",
    )(kept, came)


def finish(row_parts, column_parts, steps, tile):
    _, rows_a, size = row_parts[0].shape
    rows_b = column_parts[0].shape[1]
    count = len(row_parts)

    def kernel(*refs):
        ins, outs = refs[:-2], refs[-2:]
        for parts, out in zip((ins[:count], ins[count:]), outs):
            for s in range(steps):
                for i in range(tile):
                    total = parts[0][s * tile + i]
                    for part in parts[1:]:
                        total = total + part[s * tile + i]
                    out[:, i, s, :] = total

    outs = pl.pallas_call(
        kernel,
        in_specs=[VMEM] * (count + len(column_parts)),
        out_specs=[VMEM] * 2,
        out_shape=[
            jax.ShapeDtypeStruct((rows, tile, steps, size), jnp.float32)
            for rows in (rows_a, rows_b)
        ],
        compiler_params=pltpu.CompilerParams(vmem_limit_bytes=8 << 20),
        name="finish",
    )(*row_parts, *column_parts)
    return [out.transpose(0, 2, 1, 3) for out in outs]


def send(part, axis, flip):
    count = lax.axis_size(axis)
    return lax.ppermute(part, axis, [(at, at ^ flip) for at in range(count)])


def scatter_row(parts):
    if len(parts) == 1:
        return [lax.psum_scatter(parts[0], "ba", scatter_dimension=1, tiled=True)]
    return parts[:1] + [send(part, "ba", flip) for flip, part in enumerate(parts) if flip]


def scatter_column(parts):
    if len(parts) == 1:
        return [lax.psum_scatter(parts[0], "aa", scatter_dimension=1, tiled=True)]
    parts = list(halve(parts[0], send(parts[1], "aa", 1)))
    return parts[:1] + [send(part, "aa", 2 * at) for at, part in enumerate(parts) if at]


def gather(packed, axis):
    count = lax.axis_size(axis)
    if packed.shape[1] % 16 or count & (count - 1):
        return [lax.all_gather(packed, axis, axis=1, tiled=True)], [jnp.int32(0)]
    here = lax.axis_index(axis)
    parts, places = [packed], [here]
    for flip in range(1, count):
        parts.append(send(packed, axis, flip))
        places.append(here ^ flip)
    return parts, places


def on_device(
    pair_amplitude,
    row_amplitude,
    column_amplitude,
    row_integral,
    column_integral,
    step_integral,
    virtual_energy,
    occupied_energy,
    step_energy,
):
    tile_rows, tile_columns, tile, size = pair_amplitude.shape
    steps = row_amplitude.shape[1]
    virtual_count = tile_rows * lax.axis_size("aa")
    factor = 1.0 / (math.sqrt(virtual_count) * tile)
    packed_row, packed_column, table = pack(
        row_amplitude, column_amplitude, row_integral, column_integral, step_integral
    )
    lead_in, lead_places = gather(packed_row, "ba")
    tail_in, tail_places = gather(packed_column, "aa")
    here = [lax.axis_index("aa"), lax.axis_index("ba")]
    places = jnp.stack(here + lead_places + tail_places)
    virtual = virtual_energy.reshape(-1, math.gcd(tile_rows, tile_columns))
    table, places, virtual = lax.optimization_barrier((table, places, virtual))
    z = pair_product(table, pair_amplitude.transpose(0, 2, 1, 3), steps)
    row, column = triples(
        places, step_energy, occupied_energy, virtual, z, lead_in, tail_in, factor
    )
    return tuple(finish(scatter_row(row), scatter_column(column), steps, tile))


def solution(mesh):
    placed = (
        P("aa", "ba", None, None),
        P(("aa", "ba"), None, None, None),
        P(("ba", "aa"), None, None, None),
        P(("aa", "ba"), None),
        P(("ba", "aa"), None),
        P(),
        P(),
        P(),
        P(),
    )
    return jax.shard_map(
        on_device,
        mesh=mesh,
        in_specs=placed,
        out_specs=(P(("aa", "ba"), None, None, None), P(("ba", "aa"), None, None, None)),
        check_vma=False,
    )
```

```python
import math

import jax
import jax.numpy as jnp
from jax import lax
from jax.experimental import pallas as pl
from jax.experimental.pallas import tpu as pltpu
from jax.sharding import PartitionSpec as P

VMEM = pl.BlockSpec(memory_space=pltpu.VMEM)
SMEM = pl.BlockSpec(memory_space=pltpu.SMEM)
TRANSPOSED = (((1,), (1,)), ((), ()))


def part_by_pair(integral, turned, store, pairs, size):
    rows = integral.shape[0]
    for part in range(pairs):
        piece = integral[:, part * size : (part + 1) * size].astype(jnp.float32)
        turned[part * size : (part + 1) * size, :rows] = piece.T
    for part in range(pairs):
        store(part, turned[pl.ds(part, size, stride=pairs), :rows].T)


def pack_kernel(*refs, steps, tile, size):
    pairs = tile * tile
    given, packs, table, turned, copied, arrived = (
        refs[0:5], refs[5:7], refs[7], refs[8:11], refs[11:16], refs[16]
    )
    copies = [
        pltpu.make_async_copy(source, target, arrived.at[at])
        for at, (source, target) in enumerate(zip(given, copied))
    ]
    for copy in copies:
        copy.start()
    amplitudes, integrals, step_integral = copied[0:2], copied[2:4], copied[4]
    for side, (amplitude, integral, packed, scratch) in enumerate(
        zip(amplitudes, integrals, packs, turned)
    ):
        copies[side].wait()
        copies[2 + side].wait()
        for s in range(steps):
            for i in range(tile):
                packed[s * tile + i] = amplitude[:, i, s, :]

        def store(part, piece, packed=packed):
            packed[steps * tile + part] = piece.astype(packed.dtype)

        part_by_pair(integral, scratch, store, pairs, size)

    def store_table(part, piece):
        for s in range(steps):
            table[s * pairs + part] = piece[s].astype(table.dtype)

    copies[4].wait()
    part_by_pair(step_integral, turned[2], store_table, pairs, size)


def pack(row_amplitude, column_amplitude, row_integral, column_integral, step_integral):
    rows, steps, tile, size = row_amplitude.shape
    kinds, pairs = steps * tile + tile * tile, tile * tile
    kept = row_amplitude.dtype
    scratch = pltpu.VMEM((pairs * size, rows), jnp.float32)
    count = steps * pairs
    given = (
        row_amplitude.transpose(0, 2, 1, 3), column_amplitude.transpose(0, 2, 1, 3),
        row_integral, column_integral, step_integral,
    )
    return pl.pallas_call(
        lambda *refs: pack_kernel(*refs, steps=steps, tile=tile, size=size),
        in_specs=[pl.BlockSpec(memory_space=pltpu.HBM)] * 5,
        out_specs=[VMEM] * 3,
        out_shape=[jax.ShapeDtypeStruct((kinds, rows, size), kept)] * 2
        + [jax.ShapeDtypeStruct((count + -count % 8, size), kept)],
        scratch_shapes=[scratch, scratch, pltpu.VMEM((pairs * size, steps), jnp.float32)]
        + [pltpu.VMEM(each.shape, kept) for each in given]
        + [pltpu.SemaphoreType.DMA((5,))],
        compiler_params=pltpu.CompilerParams(vmem_limit_bytes=14 << 20),
        name="pack",
    )(*[pltpu.with_memory_space_constraint(each, pltpu.HBM) for each in given])


def pair_kernel(table, pair, out, *, count, tile, block, group):
    first = pl.program_id(0) * block
    for at in range(0, block, group):
        rows_here = pl.ds(pl.multiple_of(first + at, group), group)
        for i in range(tile):
            products = [
                lax.dot_general(
                    table[...], pair[at + row, i], TRANSPOSED, preferred_element_type=jnp.float32
                )
                for row in range(group)
            ]
            turned = jnp.swapaxes(jnp.stack(products, axis=0), 0, 1)
            out[:, i, rows_here, :] = turned[:count]


def pair_product(table, pair, steps):
    rows, tile, columns, size = pair.shape
    count = steps * tile * tile
    block, group = math.gcd(rows, 16), math.gcd(rows, 8)
    return pl.pallas_call(
        lambda *refs: pair_kernel(*refs, count=count, tile=tile, block=block, group=group),
        grid=(rows // block,),
        in_specs=[
            pl.BlockSpec(table.shape, lambda g: (0, 0)),
            pl.BlockSpec((block, tile, columns, size), lambda g: (g, 0, 0, 0)),
        ],
        out_specs=VMEM,
        out_shape=pltpu.VMEM((count, tile, rows, columns), jnp.float32),
        compiler_params=pltpu.CompilerParams(vmem_limit_bytes=14 << 20),
        name="pair_product",
    )(table, pair)


def place(parts, places, first, out):
    rows = parts[0].shape[1]
    for at, part in enumerate(parts):
        if len(parts) == 1:
            out[...] = part[...]
        else:
            start = pl.multiple_of(places[first + at] * rows, rows)
            out[:, pl.ds(start, rows), :] = part[...]


def triples_kernel(*refs, peers_a, peers_b, steps, tile, factor):
    lead_in, tail_in, refs = (
        refs[:peers_a], refs[peers_a : peers_a + peers_b], refs[peers_a + peers_b :]
    )
    places, step_energy, occupied, energies, pair = refs[:5]
    row_out, column_out, z = refs[5 : 5 + peers_a], refs[5 + peers_a : -9], refs[-9]
    (
        lead, tail, lead_turned, tail_plain, inverse, row_total, column_total, carried,
    ) = refs[-8:]
    f32 = jnp.float32
    base = steps * tile
    pairs = tile * tile

    place(lead_in, places, 2, lead)
    place(tail_in, places, 2 + peers_a, tail_plain)

    @pl.loop(0, base + pairs, unroll=tile)
    def _(e):
        tail[e] = tail_plain[e].T

    @pl.loop(0, pairs, unroll=tile)
    def _(e):
        lead_turned[e] = lead[base + e].T

    row_total[...] = jnp.zeros_like(row_total)
    column_total[...] = jnp.zeros_like(column_total)

    def slot(i, j, k):
        low = jnp.minimum(jnp.minimum(i, j), k)
        high = jnp.maximum(jnp.maximum(i, j), k)
        middle = i + j + k - low - high
        return high * (high + 1) * (high + 2) // 6 + middle * (middle + 1) // 2 + low

    def deposit(s, p):
        left = jnp.concatenate(
            [
                jnp.concatenate([lead[s * tile + w], lead[base + w * tile + p]], axis=1)
                for w in range(tile)
            ],
            axis=0,
        )
        for q in range(tile):
            right = jnp.concatenate([tail[base + p * tile + q], tail[s * tile + q]], axis=0)
            both = jnp.dot(left, right, preferred_element_type=f32)
            for w in range(tile):
                at = s * pairs + q * tile + w
                z[at, p] = pair[at, p] + both[w * rows : (w + 1) * rows]

    def forward(s, i, j):
        parts = []
        for k in range(tile):
            w = z[s * pairs + j * tile + k, i] + z[s * pairs + k * tile + i, j]
            parts.append((w * inverse[slot(i, j, k)]).astype(lead.dtype))
        return parts

    def back(parts, s, i, j):
        table = tail_plain[pl.ds(base + j * tile, tile)]
        row_total[s * tile + i] += jnp.dot(
            jnp.concatenate(parts, axis=1),
            table.reshape(tile * table.shape[1], table.shape[2]),
            preferred_element_type=f32,
        )
        column_total[s * tile + j] += jnp.dot(
            jnp.concatenate([lead_turned[k * tile + i] for k in range(tile)], axis=1),
            jnp.concatenate(parts, axis=0),
            preferred_element_type=f32,
        )

    carried[...] = jnp.zeros_like(carried)

    rows, columns = z.shape[2:]
    unit = energies.shape[1]

    def energy(first, count):
        return [energies[pl.ds(first + piece, 1), :] for piece in range(count)]

    diagonal = lax.broadcasted_iota(jnp.int32, (unit, unit), 0) == lax.broadcasted_iota(
        jnp.int32, (unit, unit), 1
    )
    upright = [
        jnp.sum(jnp.where(diagonal, piece, 0.0), axis=1, keepdims=True)
        for piece in energy(places[0] * (rows // unit), rows // unit)
    ]
    across = energy(places[1] * (columns // unit), columns // unit)
    virtual = jnp.concatenate(upright, axis=0) + jnp.concatenate(across, axis=1)

    @pl.loop(0, steps)
    def _(s):
        at = 0
        for high in range(tile):
            for middle in range(high + 1):
                for low in range(middle + 1):
                    hole = occupied[low] + occupied[middle] + occupied[high]
                    inverse[at] = 1.0 / (virtual + step_energy[s] - hole)
                    at += 1

        @pl.loop(0, tile)
        def _(p):
            deposit(s, p)

        @pl.loop(0, tile)
        def _(i):
            before = jnp.maximum(s * tile + i - 1, 0)
            waiting = [carried[k] for k in range(tile)]
            for j in range(tile):
                parts = forward(s, i, j)
                if j:
                    back(waiting, s, i, j - 1)
                else:
                    back(waiting, before // tile, before % tile, tile - 1)
                waiting = parts
            for k in range(tile):
                carried[k] = waiting[k]

    back([carried[k] for k in range(tile)], steps - 1, tile - 1, tile - 1)

    hand_out(row_total, row_out, places, 2, factor)
    if peers_b == 1:
        for e in range(base):
            column_out[0][e] = column_total[e].T * factor
        return
    rows = column_out[0].shape[2]
    here = places[2 + peers_a]

    def hand_out_columns(parity):
        @pl.loop(0, base, unroll=tile)
        def _(e):
            turned = column_total[e].T * factor
            for peer in range(peers_b):
                out = column_out[(peer + parity) % 2]
                out[(here ^ peer) // 2, e] = turned[peer * rows : (peer + 1) * rows]

    for parity in range(2):
        pl.when(here % 2 == parity)(lambda parity=parity: hand_out_columns(parity))


def hand_out(total, outs, places, first, factor):
    for at, out in enumerate(outs):
        if len(outs) == 1:
            out[...] = total[...] * factor
        else:
            rows = out.shape[1]
            start = pl.multiple_of(places[first + at] * rows, rows)
            out[...] = total[:, pl.ds(start, rows), :] * factor


def triples(places, step_energy, occupied, energies, z, lead_in, tail_in, factor):
    _, tile, rows, columns = z.shape
    steps = step_energy.shape[0]
    distinct = tile * (tile + 1) * (tile + 2) // 6
    kinds, _, size = lead_in[0].shape
    base, pairs = steps * tile, tile * tile
    f32, kept = jnp.float32, lead_in[0].dtype
    peers_a, peers_b = len(lead_in), len(tail_in)
    column_shapes = [(base, columns, size)]
    if peers_b > 1:
        column_shapes = [(peers_b // 2, base, columns // peers_b, size)] * 2
    outs = pl.pallas_call(
        lambda *refs: triples_kernel(
            *refs, peers_a=peers_a, peers_b=peers_b, steps=steps, tile=tile, factor=factor
        ),
        in_specs=[VMEM] * (peers_a + peers_b) + [SMEM] * 3 + [VMEM] * 2,
        out_specs=[VMEM] * (peers_a + len(column_shapes) + 1),
        out_shape=[jax.ShapeDtypeStruct((base, rows // peers_a, size), f32)] * peers_a
        + [jax.ShapeDtypeStruct(shape, f32) for shape in column_shapes]
        + [pltpu.VMEM(z.shape, f32)],
        input_output_aliases={peers_a + peers_b + 4: peers_a + len(column_shapes)},
        scratch_shapes=[
            pltpu.VMEM((kinds, rows, size), kept),
            pltpu.VMEM((kinds, size, columns), kept),
            pltpu.VMEM((pairs, size, rows), kept),
            pltpu.VMEM((kinds, columns, size), kept),
            pltpu.VMEM((distinct, rows, columns), f32),
            pltpu.VMEM((base, rows, size), f32),
            pltpu.VMEM((base, size, columns), f32),
            pltpu.VMEM((tile, rows, columns), kept),
        ],
        compiler_params=pltpu.CompilerParams(vmem_limit_bytes=15 << 20),
        name="triples",
    )(*lead_in, *tail_in, places, step_energy, occupied, energies, z)
    return list(outs[:peers_a]), list(outs[peers_a:-1])


def halve(kept, came):
    count = kept.shape[0]

    def kernel(kept, came, *outs):
        for at, out in enumerate(outs):
            out[...] = kept[at] + came[at]

    return pl.pallas_call(
        kernel,
        in_specs=[VMEM] * 2,
        out_specs=[VMEM] * count,
        out_shape=[jax.ShapeDtypeStruct(kept.shape[1:], kept.dtype)] * count,
        compiler_params=pltpu.CompilerParams(vmem_limit_bytes=8 << 20),
        name="halve",
    )(kept, came)


def finish(row_parts, column_parts, steps, tile):
    _, rows_a, size = row_parts[0].shape
    rows_b = column_parts[0].shape[1]
    count = len(row_parts)

    def kernel(*refs):
        ins, outs = refs[:-2], refs[-2:]
        for parts, out in zip((ins[:count], ins[count:]), outs):
            for s in range(steps):
                for i in range(tile):
                    total = parts[0][s * tile + i]
                    for part in parts[1:]:
                        total = total + part[s * tile + i]
                    out[:, i, s, :] = total

    outs = pl.pallas_call(
        kernel,
        in_specs=[VMEM] * (count + len(column_parts)),
        out_specs=[VMEM] * 2,
        out_shape=[
            jax.ShapeDtypeStruct((rows, tile, steps, size), jnp.float32)
            for rows in (rows_a, rows_b)
        ],
        compiler_params=pltpu.CompilerParams(vmem_limit_bytes=8 << 20),
        name="finish",
    )(*row_parts, *column_parts)
    return [out.transpose(0, 2, 1, 3) for out in outs]


def send(part, axis, flip):
    count = lax.axis_size(axis)
    return lax.ppermute(part, axis, [(at, at ^ flip) for at in range(count)])


def scatter_row(parts):
    if len(parts) == 1:
        return [lax.psum_scatter(parts[0], "ba", scatter_dimension=1, tiled=True)]
    return parts[:1] + [send(part, "ba", flip) for flip, part in enumerate(parts) if flip]


def scatter_column(parts):
    if len(parts) == 1:
        return [lax.psum_scatter(parts[0], "aa", scatter_dimension=1, tiled=True)]
    parts = list(halve(parts[0], send(parts[1], "aa", 1)))
    return parts[:1] + [send(part, "aa", 2 * at) for at, part in enumerate(parts) if at]


def gather(packed, axis):
    count = lax.axis_size(axis)
    if packed.shape[1] % 16 or count & (count - 1):
        return [lax.all_gather(packed, axis, axis=1, tiled=True)], [jnp.int32(0)]
    here = lax.axis_index(axis)
    parts, places = [packed], [here]
    for flip in range(1, count):
        parts.append(send(packed, axis, flip))
        places.append(here ^ flip)
    return parts, places


def on_device(
    pair_amplitude,
    row_amplitude,
    column_amplitude,
    row_integral,
    column_integral,
    step_integral,
    virtual_energy,
    occupied_energy,
    step_energy,
):
    tile_rows, tile_columns, tile, size = pair_amplitude.shape
    steps = row_amplitude.shape[1]
    virtual_count = tile_rows * lax.axis_size("aa")
    factor = 1.0 / (math.sqrt(virtual_count) * tile)
    packed_row, packed_column, table = pack(
        row_amplitude, column_amplitude, row_integral, column_integral, step_integral
    )
    lead_in, lead_places = gather(packed_row, "ba")
    tail_in, tail_places = gather(packed_column, "aa")
    here = [lax.axis_index("aa"), lax.axis_index("ba")]
    places = jnp.stack(here + lead_places + tail_places)
    virtual = virtual_energy.reshape(-1, math.gcd(tile_rows, tile_columns))
    table, places, virtual = lax.optimization_barrier((table, places, virtual))
    z = pair_product(table, pair_amplitude.transpose(0, 2, 1, 3), steps)
    row, column = triples(
        places, step_energy, occupied_energy, virtual, z, lead_in, tail_in, factor
    )
    return tuple(finish(scatter_row(row), scatter_column(column), steps, tile))


def solution(mesh):
    placed = (
        P("aa", "ba", None, None),
        P(("aa", "ba"), None, None, None),
        P(("ba", "aa"), None, None, None),
        P(("aa", "ba"), None),
        P(("ba", "aa"), None),
        P(),
        P(),
        P(),
        P(),
    )
    return jax.shard_map(
        on_device,
        mesh=mesh,
        in_specs=placed,
        out_specs=(P(("aa", "ba"), None, None, None), P(("ba", "aa"), None, None, None)),
        check_vma=False,
    )
```

```python
import math

import jax
import jax.numpy as jnp
from jax import lax
from jax.experimental import pallas as pl
from jax.experimental.pallas import tpu as pltpu
from jax.sharding import PartitionSpec as P

VMEM = pl.BlockSpec(memory_space=pltpu.VMEM)
SMEM = pl.BlockSpec(memory_space=pltpu.SMEM)
TRANSPOSED = (((1,), (1,)), ((), ()))


def part_by_pair(integral, turned, store, pairs, size):
    rows = integral.shape[0]
    for part in range(pairs):
        piece = integral[:, part * size : (part + 1) * size].astype(jnp.float32)
        turned[part * size : (part + 1) * size, :rows] = piece.T
    for part in range(pairs):
        store(part, turned[pl.ds(part, size, stride=pairs), :rows].T)


def pack_kernel(*refs, steps, tile, size):
    pairs = tile * tile
    given, packs, table, turned, copied, arrived = (
        refs[0:5], refs[5:7], refs[7], refs[8:11], refs[11:16], refs[16]
    )
    copies = [
        pltpu.make_async_copy(source, target, arrived.at[at])
        for at, (source, target) in enumerate(zip(given, copied))
    ]
    for copy in copies:
        copy.start()
    amplitudes, integrals, step_integral = copied[0:2], copied[2:4], copied[4]
    for side, (amplitude, integral, packed, scratch) in enumerate(
        zip(amplitudes, integrals, packs, turned)
    ):
        copies[side].wait()
        copies[2 + side].wait()
        for s in range(steps):
            for i in range(tile):
                packed[s * tile + i] = amplitude[:, i, s, :]

        def store(part, piece, packed=packed):
            packed[steps * tile + part] = piece.astype(packed.dtype)

        part_by_pair(integral, scratch, store, pairs, size)

    def store_table(part, piece):
        for s in range(steps):
            table[s * pairs + part] = piece[s].astype(table.dtype)

    copies[4].wait()
    part_by_pair(step_integral, turned[2], store_table, pairs, size)


def pack(row_amplitude, column_amplitude, row_integral, column_integral, step_integral):
    rows, steps, tile, size = row_amplitude.shape
    kinds, pairs = steps * tile + tile * tile, tile * tile
    kept = row_amplitude.dtype
    scratch = pltpu.VMEM((pairs * size, rows), jnp.float32)
    count = steps * pairs
    given = (
        row_amplitude.transpose(0, 2, 1, 3), column_amplitude.transpose(0, 2, 1, 3),
        row_integral, column_integral, step_integral,
    )
    return pl.pallas_call(
        lambda *refs: pack_kernel(*refs, steps=steps, tile=tile, size=size),
        in_specs=[pl.BlockSpec(memory_space=pltpu.HBM)] * 5,
        out_specs=[VMEM] * 3,
        out_shape=[jax.ShapeDtypeStruct((kinds, rows, size), kept)] * 2
        + [jax.ShapeDtypeStruct((count + -count % 8, size), kept)],
        scratch_shapes=[scratch, scratch, pltpu.VMEM((pairs * size, steps), jnp.float32)]
        + [pltpu.VMEM(each.shape, kept) for each in given]
        + [pltpu.SemaphoreType.DMA((5,))],
        compiler_params=pltpu.CompilerParams(vmem_limit_bytes=14 << 20),
        name="pack",
    )(*[pltpu.with_memory_space_constraint(each, pltpu.HBM) for each in given])


def pair_kernel(table, pair, out, *, count, tile, block, group):
    first = pl.program_id(0) * block
    for at in range(0, block, group):
        rows_here = pl.ds(pl.multiple_of(first + at, group), group)
        for i in range(tile):
            products = [
                lax.dot_general(
                    table[...], pair[at + row, i], TRANSPOSED, preferred_element_type=jnp.float32
                )
                for row in range(group)
            ]
            turned = jnp.swapaxes(jnp.stack(products, axis=0), 0, 1)
            out[:, i, rows_here, :] = turned[:count]


def pair_product(table, pair, steps):
    rows, tile, columns, size = pair.shape
    count = steps * tile * tile
    block, group = math.gcd(rows, 16), math.gcd(rows, 8)
    return pl.pallas_call(
        lambda *refs: pair_kernel(*refs, count=count, tile=tile, block=block, group=group),
        grid=(rows // block,),
        in_specs=[
            pl.BlockSpec(table.shape, lambda g: (0, 0)),
            pl.BlockSpec((block, tile, columns, size), lambda g: (g, 0, 0, 0)),
        ],
        out_specs=VMEM,
        out_shape=pltpu.VMEM((count, tile, rows, columns), jnp.float32),
        compiler_params=pltpu.CompilerParams(vmem_limit_bytes=14 << 20),
        name="pair_product",
    )(table, pair)


def place(parts, places, first, out):
    rows = parts[0].shape[1]
    for at, part in enumerate(parts):
        if len(parts) == 1:
            out[...] = part[...]
        else:
            start = pl.multiple_of(places[first + at] * rows, rows)
            out[:, pl.ds(start, rows), :] = part[...]


def triples_kernel(*refs, peers_a, peers_b, steps, tile, factor):
    lead_in, tail_in, refs = (
        refs[:peers_a], refs[peers_a : peers_a + peers_b], refs[peers_a + peers_b :]
    )
    places, step_energy, occupied, energies, pair = refs[:5]
    row_out, column_out, z = refs[5 : 5 + peers_a], refs[5 + peers_a : -10], refs[-10]
    (
        lead, tail, lead_turned, tail_plain, inverse, row_total, column_total, carried, holes,
    ) = refs[-9:]
    f32 = jnp.float32
    base = steps * tile
    pairs = tile * tile

    place(lead_in, places, 2, lead)
    place(tail_in, places, 2 + peers_a, tail_plain)

    @pl.loop(0, base, unroll=tile)
    def _(e):
        tail[e] = tail_plain[e].T

    row_total[...] = jnp.zeros_like(row_total)
    column_total[...] = jnp.zeros_like(column_total)

    def slot(i, j, k):
        low = jnp.minimum(jnp.minimum(i, j), k)
        high = jnp.maximum(jnp.maximum(i, j), k)
        middle = i + j + k - low - high
        return high * (high + 1) * (high + 2) // 6 + middle * (middle + 1) // 2 + low

    def deposit(s, p):
        left = jnp.concatenate(
            [
                jnp.concatenate([lead[s * tile + w], lead[base + w * tile + p]], axis=1)
                for w in range(tile)
            ],
            axis=0,
        )
        for m in range(distinct // tile):
            at = p * (distinct // tile) + m
            inverse[at] = 1.0 / (virtual + step_energy[s] - holes[at])
        for q in range(tile):
            lead_turned[p * tile + q] = lead[base + p * tile + q].T
            right = jnp.concatenate(
                [tail_plain[base + p * tile + q].T, tail[s * tile + q]], axis=0
            )
            both = jnp.dot(left, right, preferred_element_type=f32)
            for w in range(tile):
                at = s * pairs + q * tile + w
                z[at, p] = pair[at, p] + both[w * rows : (w + 1) * rows]

    def forward(s, i, j):
        parts = []
        for k in range(tile):
            w = z[s * pairs + j * tile + k, i] + z[s * pairs + k * tile + i, j]
            parts.append((w * inverse[slot(i, j, k)]).astype(lead.dtype))
        return parts

    def back(parts, s, i, j):
        table = tail_plain[pl.ds(base + j * tile, tile)]
        row_total[s * tile + i] += jnp.dot(
            jnp.concatenate(parts, axis=1),
            table.reshape(tile * table.shape[1], table.shape[2]),
            preferred_element_type=f32,
        )
        column_total[s * tile + j] += jnp.dot(
            jnp.concatenate([lead_turned[k * tile + i] for k in range(tile)], axis=1),
            jnp.concatenate(parts, axis=0),
            preferred_element_type=f32,
        )

    carried[...] = jnp.zeros_like(carried)

    rows, columns = z.shape[2:]
    unit = energies.shape[1]

    def energy(first, count):
        return [energies[pl.ds(first + piece, 1), :] for piece in range(count)]

    diagonal = lax.broadcasted_iota(jnp.int32, (unit, unit), 0) == lax.broadcasted_iota(
        jnp.int32, (unit, unit), 1
    )
    upright = [
        jnp.sum(jnp.where(diagonal, piece, 0.0), axis=1, keepdims=True)
        for piece in energy(places[0] * (rows // unit), rows // unit)
    ]
    across = energy(places[1] * (columns // unit), columns // unit)
    virtual = jnp.concatenate(upright, axis=0) + jnp.concatenate(across, axis=1)

    distinct = 0
    for high in range(tile):
        for middle in range(high + 1):
            for low in range(middle + 1):
                holes[distinct] = occupied[low] + occupied[middle] + occupied[high]
                distinct += 1

    @pl.loop(0, steps)
    def _(s):
        @pl.loop(0, tile)
        def _(p):
            deposit(s, p)

        @pl.loop(0, tile)
        def _(i):
            before = jnp.maximum(s * tile + i - 1, 0)
            waiting = [carried[k] for k in range(tile)]
            for j in range(tile):
                parts = forward(s, i, j)
                if j:
                    back(waiting, s, i, j - 1)
                else:
                    back(waiting, before // tile, before % tile, tile - 1)
                waiting = parts
            for k in range(tile):
                carried[k] = waiting[k]

    back([carried[k] for k in range(tile)], steps - 1, tile - 1, tile - 1)

    hand_out(row_total, row_out, places, 2, factor)
    if peers_b == 1:
        for e in range(base):
            column_out[0][e] = column_total[e].T * factor
        return
    rows = column_out[0].shape[2]
    here = places[2 + peers_a]

    def hand_out_columns(parity):
        @pl.loop(0, base, unroll=tile)
        def _(e):
            turned = column_total[e].T * factor
            for peer in range(peers_b):
                out = column_out[(peer + parity) % 2]
                out[(here ^ peer) // 2, e] = turned[peer * rows : (peer + 1) * rows]

    for parity in range(2):
        pl.when(here % 2 == parity)(lambda parity=parity: hand_out_columns(parity))


def hand_out(total, outs, places, first, factor):
    for at, out in enumerate(outs):
        if len(outs) == 1:
            out[...] = total[...] * factor
        else:
            rows = out.shape[1]
            start = pl.multiple_of(places[first + at] * rows, rows)
            out[...] = total[:, pl.ds(start, rows), :] * factor


def triples(places, step_energy, occupied, energies, z, lead_in, tail_in, factor):
    _, tile, rows, columns = z.shape
    steps = step_energy.shape[0]
    distinct = tile * (tile + 1) * (tile + 2) // 6
    kinds, _, size = lead_in[0].shape
    base, pairs = steps * tile, tile * tile
    f32, kept = jnp.float32, lead_in[0].dtype
    peers_a, peers_b = len(lead_in), len(tail_in)
    column_shapes = [(base, columns, size)]
    if peers_b > 1:
        column_shapes = [(peers_b // 2, base, columns // peers_b, size)] * 2
    outs = pl.pallas_call(
        lambda *refs: triples_kernel(
            *refs, peers_a=peers_a, peers_b=peers_b, steps=steps, tile=tile, factor=factor
        ),
        in_specs=[VMEM] * (peers_a + peers_b) + [SMEM] * 3 + [VMEM] * 2,
        out_specs=[VMEM] * (peers_a + len(column_shapes) + 1),
        out_shape=[jax.ShapeDtypeStruct((base, rows // peers_a, size), f32)] * peers_a
        + [jax.ShapeDtypeStruct(shape, f32) for shape in column_shapes]
        + [pltpu.VMEM(z.shape, f32)],
        input_output_aliases={peers_a + peers_b + 4: peers_a + len(column_shapes)},
        scratch_shapes=[
            pltpu.VMEM((kinds, rows, size), kept),
            pltpu.VMEM((base, size, columns), kept),
            pltpu.VMEM((pairs, size, rows), kept),
            pltpu.VMEM((kinds, columns, size), kept),
            pltpu.VMEM((distinct, rows, columns), f32),
            pltpu.VMEM((base, rows, size), f32),
            pltpu.VMEM((base, size, columns), f32),
            pltpu.VMEM((tile, rows, columns), kept),
            pltpu.SMEM((distinct,), f32),
        ],
        compiler_params=pltpu.CompilerParams(vmem_limit_bytes=15 << 20),
        name="triples",
    )(*lead_in, *tail_in, places, step_energy, occupied, energies, z)
    return list(outs[:peers_a]), list(outs[peers_a:-1])


def halve(kept, came):
    count = kept.shape[0]

    def kernel(kept, came, *outs):
        for at, out in enumerate(outs):
            out[...] = kept[at] + came[at]

    return pl.pallas_call(
        kernel,
        in_specs=[VMEM] * 2,
        out_specs=[VMEM] * count,
        out_shape=[jax.ShapeDtypeStruct(kept.shape[1:], kept.dtype)] * count,
        compiler_params=pltpu.CompilerParams(vmem_limit_bytes=8 << 20),
        name="halve",
    )(kept, came)


def finish(row_parts, column_parts, steps, tile):
    _, rows_a, size = row_parts[0].shape
    rows_b = column_parts[0].shape[1]
    count = len(row_parts)

    def kernel(*refs):
        ins, outs = refs[:-2], refs[-2:]
        for parts, out in zip((ins[:count], ins[count:]), outs):
            for s in range(steps):
                for i in range(tile):
                    total = parts[0][s * tile + i]
                    for part in parts[1:]:
                        total = total + part[s * tile + i]
                    out[:, i, s, :] = total

    outs = pl.pallas_call(
        kernel,
        in_specs=[VMEM] * (count + len(column_parts)),
        out_specs=[VMEM] * 2,
        out_shape=[
            jax.ShapeDtypeStruct((rows, tile, steps, size), jnp.float32)
            for rows in (rows_a, rows_b)
        ],
        compiler_params=pltpu.CompilerParams(vmem_limit_bytes=8 << 20),
        name="finish",
    )(*row_parts, *column_parts)
    return [out.transpose(0, 2, 1, 3) for out in outs]


def send(part, axis, flip):
    count = lax.axis_size(axis)
    return lax.ppermute(part, axis, [(at, at ^ flip) for at in range(count)])


def scatter_row(parts):
    if len(parts) == 1:
        return [lax.psum_scatter(parts[0], "ba", scatter_dimension=1, tiled=True)]
    return parts[:1] + [send(part, "ba", flip) for flip, part in enumerate(parts) if flip]


def scatter_column(parts):
    if len(parts) == 1:
        return [lax.psum_scatter(parts[0], "aa", scatter_dimension=1, tiled=True)]
    parts = list(halve(parts[0], send(parts[1], "aa", 1)))
    return parts[:1] + [send(part, "aa", 2 * at) for at, part in enumerate(parts) if at]


def gather(packed, axis):
    count = lax.axis_size(axis)
    if packed.shape[1] % 16 or count & (count - 1):
        return [lax.all_gather(packed, axis, axis=1, tiled=True)], [jnp.int32(0)]
    here = lax.axis_index(axis)
    parts, places = [packed], [here]
    for flip in range(1, count):
        parts.append(send(packed, axis, flip))
        places.append(here ^ flip)
    return parts, places


def on_device(
    pair_amplitude,
    row_amplitude,
    column_amplitude,
    row_integral,
    column_integral,
    step_integral,
    virtual_energy,
    occupied_energy,
    step_energy,
):
    tile_rows, tile_columns, tile, size = pair_amplitude.shape
    steps = row_amplitude.shape[1]
    virtual_count = tile_rows * lax.axis_size("aa")
    factor = 1.0 / (math.sqrt(virtual_count) * tile)
    packed_row, packed_column, table = pack(
        row_amplitude, column_amplitude, row_integral, column_integral, step_integral
    )
    lead_in, lead_places = gather(packed_row, "ba")
    tail_in, tail_places = gather(packed_column, "aa")
    here = [lax.axis_index("aa"), lax.axis_index("ba")]
    places = jnp.stack(here + lead_places + tail_places)
    virtual = virtual_energy.reshape(-1, math.gcd(tile_rows, tile_columns))
    table, places, virtual = lax.optimization_barrier((table, places, virtual))
    z = pair_product(table, pair_amplitude.transpose(0, 2, 1, 3), steps)
    row, column = triples(
        places, step_energy, occupied_energy, virtual, z, lead_in, tail_in, factor
    )
    return tuple(finish(scatter_row(row), scatter_column(column), steps, tile))


def solution(mesh):
    placed = (
        P("aa", "ba", None, None),
        P(("aa", "ba"), None, None, None),
        P(("ba", "aa"), None, None, None),
        P(("aa", "ba"), None),
        P(("ba", "aa"), None),
        P(),
        P(),
        P(),
        P(),
    )
    return jax.shard_map(
        on_device,
        mesh=mesh,
        in_specs=placed,
        out_specs=(P(("aa", "ba"), None, None, None), P(("ba", "aa"), None, None, None)),
        check_vma=False,
    )
```

```python
import math

import jax
import jax.numpy as jnp
from jax import lax
from jax.experimental import pallas as pl
from jax.experimental.pallas import tpu as pltpu
from jax.sharding import PartitionSpec as P

VMEM = pl.BlockSpec(memory_space=pltpu.VMEM)
SMEM = pl.BlockSpec(memory_space=pltpu.SMEM)
TRANSPOSED = (((1,), (1,)), ((), ()))


def part_by_pair(integrals, turned, stores, pairs, size):
    ends = [0]
    for integral in integrals:
        ends.append(ends[-1] + integral.shape[0])
    for part in range(pairs):
        pieces = [
            integral[:, part * size : (part + 1) * size].astype(jnp.float32)
            for integral in integrals
        ]
        turned[part * size : (part + 1) * size, : ends[-1]] = jnp.concatenate(pieces, axis=0).T
    for part in range(pairs):
        piece = turned[pl.ds(part, size, stride=pairs), : ends[-1]].T
        for store, start, end in zip(stores, ends, ends[1:]):
            store(part, piece[start:end])


def pack_kernel(*refs, steps, tile, size):
    pairs = tile * tile
    given, packs, table, turned, copied, arrived = (
        refs[0:5], refs[5:7], refs[7], refs[8], refs[9:14], refs[14]
    )
    copies = [
        pltpu.make_async_copy(source, target, arrived.at[at])
        for at, (source, target) in enumerate(zip(given, copied))
    ]
    for copy in copies:
        copy.start()
    for copy in copies:
        copy.wait()
    stores = []
    for amplitude, packed in zip(copied[0:2], packs):
        for s in range(steps):
            for i in range(tile):
                packed[s * tile + i] = amplitude[:, i, s, :]

        def store(part, piece, packed=packed):
            packed[steps * tile + part] = piece.astype(packed.dtype)

        stores.append(store)

    def store_table(part, piece):
        for s in range(steps):
            table[s * pairs + part] = piece[s].astype(table.dtype)

    stores.append(store_table)
    integrals = copied[2:5]
    if integrals[0].shape[0] % 16:
        for integral, store in zip(integrals, stores):
            part_by_pair([integral], turned, [store], pairs, size)
    else:
        part_by_pair(integrals, turned, stores, pairs, size)


def pack(row_amplitude, column_amplitude, row_integral, column_integral, step_integral):
    rows, steps, tile, size = row_amplitude.shape
    kinds, pairs = steps * tile + tile * tile, tile * tile
    kept = row_amplitude.dtype
    scratch = pltpu.VMEM((pairs * size, 2 * rows + steps), jnp.float32)
    count = steps * pairs
    given = (
        row_amplitude.transpose(0, 2, 1, 3), column_amplitude.transpose(0, 2, 1, 3),
        row_integral, column_integral, step_integral,
    )
    return pl.pallas_call(
        lambda *refs: pack_kernel(*refs, steps=steps, tile=tile, size=size),
        in_specs=[pl.BlockSpec(memory_space=pltpu.HBM)] * 5,
        out_specs=[VMEM] * 3,
        out_shape=[jax.ShapeDtypeStruct((kinds, rows, size), kept)] * 2
        + [jax.ShapeDtypeStruct((count + -count % 8, size), kept)],
        scratch_shapes=[scratch]
        + [pltpu.VMEM(each.shape, kept) for each in given]
        + [pltpu.SemaphoreType.DMA((5,))],
        compiler_params=pltpu.CompilerParams(vmem_limit_bytes=14 << 20),
        name="pack",
    )(*[pltpu.with_memory_space_constraint(each, pltpu.HBM) for each in given])


def pair_kernel(table, pair, out, *, count, tile, block, group):
    first = pl.program_id(0) * block
    for at in range(0, block, group):
        rows_here = pl.ds(pl.multiple_of(first + at, group), group)
        for i in range(tile):
            products = [
                lax.dot_general(
                    table[...], pair[at + row, i], TRANSPOSED, preferred_element_type=jnp.float32
                )
                for row in range(group)
            ]
            turned = jnp.swapaxes(jnp.stack(products, axis=0), 0, 1)
            out[:, i, rows_here, :] = turned[:count]


def pair_product(table, pair, steps):
    rows, tile, columns, size = pair.shape
    count = steps * tile * tile
    block, group = math.gcd(rows, 16), math.gcd(rows, 8)
    return pl.pallas_call(
        lambda *refs: pair_kernel(*refs, count=count, tile=tile, block=block, group=group),
        grid=(rows // block,),
        in_specs=[
            pl.BlockSpec(table.shape, lambda g: (0, 0)),
            pl.BlockSpec((block, tile, columns, size), lambda g: (g, 0, 0, 0)),
        ],
        out_specs=VMEM,
        out_shape=pltpu.VMEM((count, tile, rows, columns), jnp.float32),
        compiler_params=pltpu.CompilerParams(vmem_limit_bytes=14 << 20),
        name="pair_product",
    )(table, pair)


def place(parts, places, first, out):
    rows = parts[0].shape[1]
    for at, part in enumerate(parts):
        if len(parts) == 1:
            out[...] = part[...]
        else:
            start = pl.multiple_of(places[first + at] * rows, rows)
            out[:, pl.ds(start, rows), :] = part[...]


def triples_kernel(*refs, peers_a, peers_b, steps, tile, factor):
    lead_in, tail_in, refs = (
        refs[:peers_a], refs[peers_a : peers_a + peers_b], refs[peers_a + peers_b :]
    )
    places, step_energy, occupied, energies, pair = refs[:5]
    row_out, column_out, z = refs[5 : 5 + peers_a], refs[5 + peers_a : -10], refs[-10]
    (
        lead, tail, lead_turned, tail_plain, inverse, row_total, column_total, carried, holes,
    ) = refs[-9:]
    f32 = jnp.float32
    base = steps * tile
    pairs = tile * tile

    place(lead_in, places, 2, lead)
    place(tail_in, places, 2 + peers_a, tail_plain)

    @pl.loop(0, base, unroll=tile)
    def _(e):
        tail[e] = tail_plain[e].T

    row_total[...] = jnp.zeros_like(row_total)
    column_total[...] = jnp.zeros_like(column_total)

    def slot(i, j, k):
        low = jnp.minimum(jnp.minimum(i, j), k)
        high = jnp.maximum(jnp.maximum(i, j), k)
        middle = i + j + k - low - high
        return high * (high + 1) * (high + 2) // 6 + middle * (middle + 1) // 2 + low

    def deposit(s, p):
        left = jnp.concatenate(
            [
                jnp.concatenate([lead[s * tile + w], lead[base + w * tile + p]], axis=1)
                for w in range(tile)
            ],
            axis=0,
        )
        for m in range(distinct // tile):
            at = p * (distinct // tile) + m
            inverse[at] = 1.0 / (virtual + step_energy[s] - holes[at])
        for q in range(tile):
            lead_turned[p * tile + q] = lead[base + p * tile + q].T
            right = jnp.concatenate(
                [tail_plain[base + p * tile + q].T, tail[s * tile + q]], axis=0
            )
            both = jnp.dot(left, right, preferred_element_type=f32)
            for w in range(tile):
                at = s * pairs + q * tile + w
                z[at, p] = pair[at, p] + both[w * rows : (w + 1) * rows]

    def forward(s, i, j):
        parts = []
        for k in range(tile):
            w = z[s * pairs + j * tile + k, i] + z[s * pairs + k * tile + i, j]
            parts.append((w * inverse[slot(i, j, k)]).astype(lead.dtype))
        return parts

    def back(parts, s, i, j):
        table = tail_plain[pl.ds(base + j * tile, tile)]
        row_total[s * tile + i] += jnp.dot(
            jnp.concatenate(parts, axis=1),
            table.reshape(tile * table.shape[1], table.shape[2]),
            preferred_element_type=f32,
        )
        column_total[s * tile + j] += jnp.dot(
            jnp.concatenate([lead_turned[k * tile + i] for k in range(tile)], axis=1),
            jnp.concatenate(parts, axis=0),
            preferred_element_type=f32,
        )

    carried[...] = jnp.zeros_like(carried)

    rows, columns = z.shape[2:]
    unit = energies.shape[1]

    def energy(first, count):
        return [energies[pl.ds(first + piece, 1), :] for piece in range(count)]

    diagonal = lax.broadcasted_iota(jnp.int32, (unit, unit), 0) == lax.broadcasted_iota(
        jnp.int32, (unit, unit), 1
    )
    upright = [
        jnp.sum(jnp.where(diagonal, piece, 0.0), axis=1, keepdims=True)
        for piece in energy(places[0] * (rows // unit), rows // unit)
    ]
    across = energy(places[1] * (columns // unit), columns // unit)
    virtual = jnp.concatenate(upright, axis=0) + jnp.concatenate(across, axis=1)

    distinct = 0
    for high in range(tile):
        for middle in range(high + 1):
            for low in range(middle + 1):
                holes[distinct] = occupied[low] + occupied[middle] + occupied[high]
                distinct += 1

    @pl.loop(0, steps)
    def _(s):
        @pl.loop(0, tile, unroll=tile)
        def _(p):
            deposit(s, p)

        @pl.loop(0, tile, unroll=tile)
        def _(i):
            before = jnp.maximum(s * tile + i - 1, 0)
            waiting = [carried[k] for k in range(tile)]
            for j in range(tile):
                parts = forward(s, i, j)
                if j:
                    back(waiting, s, i, j - 1)
                else:
                    back(waiting, before // tile, before % tile, tile - 1)
                waiting = parts
            for k in range(tile):
                carried[k] = waiting[k]

    back([carried[k] for k in range(tile)], steps - 1, tile - 1, tile - 1)

    hand_out(row_total, row_out, places, 2, factor)
    if peers_b == 1:
        for e in range(base):
            column_out[0][e] = column_total[e].T * factor
        return
    rows = column_out[0].shape[2]
    here = places[2 + peers_a]

    def hand_out_columns(parity):
        @pl.loop(0, base, unroll=tile)
        def _(e):
            turned = column_total[e].T * factor
            for peer in range(peers_b):
                out = column_out[(peer + parity) % 2]
                out[(here ^ peer) // 2, e] = turned[peer * rows : (peer + 1) * rows]

    for parity in range(2):
        pl.when(here % 2 == parity)(lambda parity=parity: hand_out_columns(parity))


def hand_out(total, outs, places, first, factor):
    for at, out in enumerate(outs):
        if len(outs) == 1:
            out[...] = total[...] * factor
        else:
            rows = out.shape[1]
            start = pl.multiple_of(places[first + at] * rows, rows)
            out[...] = total[:, pl.ds(start, rows), :] * factor


def triples(places, step_energy, occupied, energies, z, lead_in, tail_in, factor):
    _, tile, rows, columns = z.shape
    steps = step_energy.shape[0]
    distinct = tile * (tile + 1) * (tile + 2) // 6
    kinds, _, size = lead_in[0].shape
    base, pairs = steps * tile, tile * tile
    f32, kept = jnp.float32, lead_in[0].dtype
    peers_a, peers_b = len(lead_in), len(tail_in)
    column_shapes = [(base, columns, size)]
    if peers_b > 1:
        column_shapes = [(peers_b // 2, base, columns // peers_b, size)] * 2
    outs = pl.pallas_call(
        lambda *refs: triples_kernel(
            *refs, peers_a=peers_a, peers_b=peers_b, steps=steps, tile=tile, factor=factor
        ),
        in_specs=[VMEM] * (peers_a + peers_b) + [SMEM] * 3 + [VMEM] * 2,
        out_specs=[VMEM] * (peers_a + len(column_shapes) + 1),
        out_shape=[jax.ShapeDtypeStruct((base, rows // peers_a, size), f32)] * peers_a
        + [jax.ShapeDtypeStruct(shape, f32) for shape in column_shapes]
        + [pltpu.VMEM(z.shape, f32)],
        input_output_aliases={peers_a + peers_b + 4: peers_a + len(column_shapes)},
        scratch_shapes=[
            pltpu.VMEM((kinds, rows, size), kept),
            pltpu.VMEM((base, size, columns), kept),
            pltpu.VMEM((pairs, size, rows), kept),
            pltpu.VMEM((kinds, columns, size), kept),
            pltpu.VMEM((distinct, rows, columns), f32),
            pltpu.VMEM((base, rows, size), f32),
            pltpu.VMEM((base, size, columns), f32),
            pltpu.VMEM((tile, rows, columns), kept),
            pltpu.SMEM((distinct,), f32),
        ],
        compiler_params=pltpu.CompilerParams(vmem_limit_bytes=15 << 20),
        name="triples",
    )(*lead_in, *tail_in, places, step_energy, occupied, energies, z)
    return list(outs[:peers_a]), list(outs[peers_a:-1])


def halve(kept, came):
    count = kept.shape[0]

    def kernel(kept, came, *outs):
        for at, out in enumerate(outs):
            out[...] = kept[at] + came[at]

    return pl.pallas_call(
        kernel,
        in_specs=[VMEM] * 2,
        out_specs=[VMEM] * count,
        out_shape=[jax.ShapeDtypeStruct(kept.shape[1:], kept.dtype)] * count,
        compiler_params=pltpu.CompilerParams(vmem_limit_bytes=8 << 20),
        name="halve",
    )(kept, came)


def finish(row_parts, column_parts, steps, tile):
    _, rows_a, size = row_parts[0].shape
    rows_b = column_parts[0].shape[1]
    count = len(row_parts)

    def kernel(*refs):
        ins, outs = refs[:-2], refs[-2:]
        for parts, out in zip((ins[:count], ins[count:]), outs):
            for s in range(steps):
                for i in range(tile):
                    total = parts[0][s * tile + i]
                    for part in parts[1:]:
                        total = total + part[s * tile + i]
                    out[:, i, s, :] = total

    outs = pl.pallas_call(
        kernel,
        in_specs=[VMEM] * (count + len(column_parts)),
        out_specs=[VMEM] * 2,
        out_shape=[
            jax.ShapeDtypeStruct((rows, tile, steps, size), jnp.float32)
            for rows in (rows_a, rows_b)
        ],
        compiler_params=pltpu.CompilerParams(vmem_limit_bytes=8 << 20),
        name="finish",
    )(*row_parts, *column_parts)
    return [out.transpose(0, 2, 1, 3) for out in outs]


def send(part, axis, flip):
    count = lax.axis_size(axis)
    return lax.ppermute(part, axis, [(at, at ^ flip) for at in range(count)])


def scatter_row(parts):
    if len(parts) == 1:
        return [lax.psum_scatter(parts[0], "ba", scatter_dimension=1, tiled=True)]
    return parts[:1] + [send(part, "ba", flip) for flip, part in enumerate(parts) if flip]


def scatter_column(parts):
    if len(parts) == 1:
        return [lax.psum_scatter(parts[0], "aa", scatter_dimension=1, tiled=True)]
    parts = list(halve(parts[0], send(parts[1], "aa", 1)))
    return parts[:1] + [send(part, "aa", 2 * at) for at, part in enumerate(parts) if at]


def gather(packed, axis):
    count = lax.axis_size(axis)
    if packed.shape[1] % 16 or count & (count - 1):
        return [lax.all_gather(packed, axis, axis=1, tiled=True)], [jnp.int32(0)]
    here = lax.axis_index(axis)
    parts, places = [packed], [here]
    for flip in range(1, count):
        parts.append(send(packed, axis, flip))
        places.append(here ^ flip)
    return parts, places


def on_device(
    pair_amplitude,
    row_amplitude,
    column_amplitude,
    row_integral,
    column_integral,
    step_integral,
    virtual_energy,
    occupied_energy,
    step_energy,
):
    tile_rows, tile_columns, tile, size = pair_amplitude.shape
    steps = row_amplitude.shape[1]
    virtual_count = tile_rows * lax.axis_size("aa")
    factor = 1.0 / (math.sqrt(virtual_count) * tile)
    packed_row, packed_column, table = pack(
        row_amplitude, column_amplitude, row_integral, column_integral, step_integral
    )
    lead_in, lead_places = gather(packed_row, "ba")
    tail_in, tail_places = gather(packed_column, "aa")
    here = [lax.axis_index("aa"), lax.axis_index("ba")]
    places = jnp.stack(here + lead_places + tail_places)
    virtual = virtual_energy.reshape(-1, math.gcd(tile_rows, tile_columns))
    table, places, virtual = lax.optimization_barrier((table, places, virtual))
    z = pair_product(table, pair_amplitude.transpose(0, 2, 1, 3), steps)
    row, column = triples(
        places, step_energy, occupied_energy, virtual, z, lead_in, tail_in, factor
    )
    return tuple(finish(scatter_row(row), scatter_column(column), steps, tile))


def solution(mesh):
    placed = (
        P("aa", "ba", None, None),
        P(("aa", "ba"), None, None, None),
        P(("ba", "aa"), None, None, None),
        P(("aa", "ba"), None),
        P(("ba", "aa"), None),
        P(),
        P(),
        P(),
        P(),
    )
    return jax.shard_map(
        on_device,
        mesh=mesh,
        in_specs=placed,
        out_specs=(P(("aa", "ba"), None, None, None), P(("ba", "aa"), None, None, None)),
        check_vma=False,
    )
```
